32 devices in a mesh: col: 8 (over z, core), row: 4 (over y, x).
Axes of the slice: x: 2, y: 2, z: 4, core: 2. Of those that a mesh axis runs over, the one named last changes fastest.
Arguments:
- matrix: float32 [4096, 4096], P('row', 'col'), may hold values from -64 to 64, as said below
- plan: int32 [3, 8], replicated, may hold values from 0 to 1
Outputs:
- rotated: float32 [4096, 4096], P('row', 'col')
- coupling: float32 [3], replicated
The draws below stay inside these ranges and needn't reach their ends.
Inputs may be any that keep to these rules, and one draw needn't show every extreme that they name: Entries of the matrix are real numbers; column scales differ between columns.
All inputs are finite; a program needn't handle non-finite values.
Results may differ from the reference program's by a relative error of at most 0.0003.
Values sent between devices are 32-bit elements; how exact they have to be, the bound alone decides.
A program may use at most 128 MiB of HBM per device.

```python
import jax
import jax.numpy as jnp
from jax import lax

BLOCK = 256
SWEEPS = 2
STEPS = 3
ROWS = 4096
COLS = 4096
N_COL = 8


def draw_matrix(key, part):
    key_base = jax.random.fold_in(key, 11)
    key_cols = jax.random.fold_in(key, 12)
    column = jnp.arange(COLS).astype(jnp.float32)
    rising = 1.0 + 3.0 * column / COLS
    rough = jnp.exp(jax.random.uniform(key_cols, (COLS,), jnp.float32, -0.7, 0.7))
    base = jnp.clip(jax.random.normal(key_base, (ROWS, COLS), jnp.float32), -6.0, 6.0)
    values = base * (rough * rising)[None, :]
    return jnp.clip(values, -64.0, 64.0)


def set_ends(array, key, least, largest):
    index_at = [jax.random.randint(jax.random.fold_in(key, axis), (), 0, length) for axis, length in enumerate(array.shape)]
    longest = array.shape.index(max(array.shape))
    neighbour = index_at[:longest] + [(index_at[longest] + 1) % array.shape[longest]] + index_at[longest + 1:]
    return array.at[tuple(index_at)].set(least).at[tuple(neighbour)].set(largest)


def setup_inputs(seed: int = 0) -> dict:
    key_list = jax.random.split(jax.random.key(seed), 3)
    return {
        "matrix": draw_matrix(jax.random.fold_in(key_list[2], 71), 0),
        "plan": set_ends(jax.random.randint(key_list[1], (STEPS, N_COL), 0, 2), jax.random.fold_in(key_list[1], 1), 0, 1).astype(jnp.int32),
    }


highest = lax.Precision.HIGHEST
eps = 1e-06

def product(first, second):
    return jnp.dot(first, second, precision=highest, preferred_element_type=jnp.float32)

def sweep_rotation(gram):
    width = gram.shape[0]
    eye = jnp.eye(width, dtype=jnp.float32)
    upper = jnp.triu(jnp.ones((width, width), jnp.float32), 1)
    rotation = eye
    for sweep in range(SWEEPS):
        diag = jnp.diagonal(gram)
        ratio = gram / (diag[:, None] + diag[None, :] + eps) * upper
        skew_raw = ratio - ratio.T
        scale = jnp.maximum(jnp.sqrt(jnp.sum(skew_raw * skew_raw)), 1.0)
        skew = skew_raw / scale
        square = product(skew, skew)
        system = eye - square
        inverse = 4.0 / 3.0 * eye - 4.0 / 9.0 * system
        for turn in range(2):
            inverse = product(inverse, 2.0 * eye - product(system, inverse))
        qmat = product(eye - 2.0 * skew + square, inverse)
        gram = product(qmat.T, product(gram, qmat))
        if sweep == 0:
            rotation = qmat
        else:
            rotation = product(rotation, qmat)
    return (rotation, gram)

def rotate_pair(pair):
    gram = lax.dot_general(pair, pair, (((0,), (0,)), ((), ())), precision=highest, preferred_element_type=jnp.float32)
    rotation, turned = sweep_rotation(gram)
    moved = product(pair, rotation)
    cross_sq = jnp.sum(turned[:BLOCK, BLOCK:] * turned[:BLOCK, BLOCK:])
    diag_sq = jnp.sum(jnp.diagonal(turned) ** 2)
    return (moved, cross_sq, diag_sq)

def reference(matrix, plan):
    pairs = matrix.reshape(ROWS, N_COL, 2 * BLOCK).transpose(1, 0, 2)
    values = []
    for step in range(STEPS):
        moved, cross_sq, diag_sq = lax.map(rotate_pair, pairs)
        values.append(jnp.log(jnp.sum(cross_sq) / jnp.sum(diag_sq)))
        left = moved[:, :, :BLOCK]
        right = moved[:, :, BLOCK:]
        flag = (plan[step] == 1)[:, None, None]
        send = jnp.where(flag, right, left)
        keep = jnp.where(flag, left, right)
        received = jnp.roll(send, 1, axis=0)
        pairs = jnp.concatenate([keep, received], axis=2)
    rotated = pairs.transpose(1, 0, 2).reshape(ROWS, COLS)
    return (rotated, jnp.stack(values).astype(jnp.float32))
```

```python
import functools

import jax
import jax.numpy as jnp
from jax import lax
from jax.experimental import pallas as pl
from jax.experimental.pallas import tpu as pltpu
from jax.sharding import PartitionSpec as P

SWEEPS = 2
STEPS = 3
MESH = pl.DeviceIdType.MESH
f32 = jnp.float32
bf16 = jnp.bfloat16
eps = 1e-06
COEF = tuple(c / 6561.0 for c in (6560.0, 6544.0, 6432.0, 5984.0, 4864.0, 3072.0, 1280.0, 256.0))


def split(x):
    big = x.astype(bf16)
    return big, (x - big.astype(f32)).astype(bf16)


def dot1(a, b):
    return jnp.dot(a, b, preferred_element_type=f32)


def dot3(a, b):
    return dot1(a[0], b[0]) + (dot1(a[0], b[1]) + dot1(a[1], b[0]))


def sweep(gram, row, column):
    on_diag = row == column
    only = jnp.where(on_diag, gram, 0.0)
    d_row = jnp.sum(only, axis=0, keepdims=True)
    d_col = jnp.sum(only, axis=1, keepdims=True)
    ratio = gram / (d_col + d_row + eps)
    raw = jnp.where(row < column, ratio, jnp.where(row > column, -ratio, 0.0))
    scale = jnp.maximum(jnp.sqrt(jnp.sum(raw * raw, keepdims=True)), 1.0)
    skew = raw / scale
    parts = split(skew)
    a1 = dot1(parts[0], parts[0])
    a1b = a1.astype(bf16)
    a2 = dot1(a1b, a1b)
    a2b = a2.astype(bf16)
    a3 = dot1(a1b, a2b)
    a4 = dot1(a2b, a2b)
    low = COEF[5] * a1 + COEF[6] * a2 + COEF[7] * a3
    tail = dot1(a4.astype(bf16), low.astype(bf16))
    above = COEF[1] * a1 + COEF[2] * a2 + COEF[3] * a3 + (COEF[4] * a4 + tail)
    factor = a1 - 2.0 * skew
    extra = above + COEF[0] * factor + dot1(factor.astype(bf16), above.astype(bf16))
    extra = extra + jnp.where(on_diag, COEF[0] - 1.0, 0.0)
    part = split(extra)
    half = gram + dot3(split(gram), part)
    return extra, part, half


def finish_turn(extra, half):
    return half + dot3(split(extra.T), split(half))


def tall(first, second):
    def one(a, b):
        return lax.dot_general(a, b, (((0,), (0,)), ((), ())), preferred_element_type=f32)

    return one(first[0], second[0]) + (one(first[0], second[1]) + one(first[1], second[0]))


def remote(src, dst, send, recv, where):
    return pltpu.make_async_remote_copy(
        src_ref=src, dst_ref=dst, send_sem=send, recv_sem=recv, device_id=where, device_id_type=MESH
    )


def turn_stats(turned, row, column):
    block = turned.shape[0] // 2
    off = turned[:block, block:]
    only = jnp.where(row == column, turned[...], 0.0)
    cross_sq = jnp.sum(off * off, keepdims=True)
    diag_sq = jnp.sum(only * only, keepdims=True)
    lane = lax.broadcasted_iota(jnp.int32, (1, 128), 1)
    return jnp.where(lane == 0, cross_sq, jnp.where(lane == 1, diag_sq, 0.0))


def whole_kernel(cols, rows, chunk, flag_ref, pair_ref, out_ref, sums_ref,
                 g, total, extra, half, turned, ph, pm, nh, nm,
                 near0, near_in, s_send, vs_send, vs_in, vk_send, vk_in, gs_send, gs_in,
                 local, got, cross, glocal, ggot, gup, mine_stat, got_stat,
                 near_sem, s_sem, vs_sem, vk_sem, gs_sem, ra_sem, rb_sem, ga_sem, gb_sem, st_sem):
    width = g.shape[0]
    block = width // 2
    pieces = block // chunk
    last = STEPS - 1
    col = lax.axis_index("col")
    me = lax.axis_index("row")
    right = {"col": lax.rem(col + 1, cols)}
    peers = [lax.rem(me + k, rows) for k in range(1, rows)]
    row = lax.broadcasted_iota(jnp.int32, (width, width), 0)
    column = lax.broadcasted_iota(jnp.int32, (width, width), 1)
    pending = []

    def share(who, size):
        return pl.ds(pl.multiple_of(who * size, size), size)

    def launch(src, dst, sems, at, where):
        copy = remote(src, dst, sems.at[(0,) + at], sems.at[(1,) + at], where)
        copy.start()
        pending.append(copy)
        return copy

    barrier = pltpu.get_barrier_semaphore()
    for k in range(1, cols):
        pl.semaphore_signal(barrier, inc=1, device_id={"col": lax.rem(col + k, cols)}, device_id_type=MESH)
    for peer in peers:
        pl.semaphore_signal(barrier, inc=1, device_id={"row": peer}, device_id_type=MESH)

    ph[...], pm[...] = split(pair_ref[...])
    tiles = width // chunk
    scatter = {}
    order = list(range(tiles))[::-1]
    for n, k in enumerate(order):
        high = (k + 1) * chunk
        at = slice(k * chunk, high)
        glocal[k, :high] = tall((ph[:, :high], pm[:, :high]), (ph[:, at], pm[:, at]))
        if n == 0:
            pl.semaphore_wait(barrier, cols + rows - 2)
        for i, peer in enumerate(peers):
            scatter[k, i] = launch(glocal.at[k, share(peer, high // rows)], ggot.at[k, i, : high // rows],
                                   ga_sem, (k, i), {"row": peer})
        if n == 0:
            near_copy = launch(pair_ref, near0, near_sem, (0,), right)
    gather = []
    for k in order:
        high = (k + 1) * chunk
        mine = share(me, high // rows)
        at = slice(k * chunk, high)
        sumd = glocal[k, mine]
        for i in range(rows - 1):
            scatter[k, i].wait_recv()
            sumd = sumd + ggot[k, i, : high // rows]
        gup[mine, at] = sumd
        for i, peer in enumerate(peers):
            spot = gup.at[mine, at]
            gather.append(launch(spot, spot, gb_sem, (k, i), {"row": peer}))
    for copy in gather:
        copy.wait_recv()
    for k in range(tiles):
        at = slice(k * chunk, (k + 1) * chunk)
        for j in range(k + 1):
            to = slice(j * chunk, (j + 1) * chunk)
            tile = gup[to, at]
            g[to, at] = tile
            if j < k:
                g[at, to] = tile.T

    def step(s):
        first, part, first_half = sweep(g[...], row, column)
        total[...] = first
        extra[...] = first
        half[...] = first_half
        for turn in range(1, SWEEPS):
            g[...] = finish_turn(extra[...], half[...])
            more, part, more_half = sweep(g[...], row, column)
            before = total[...]
            total[...] = before + more + dot1(before.astype(bf16), part[0])
            extra[...] = more
            half[...] = more_half
        rotation = total[...] + jnp.where(row == column, 1.0, 0.0)
        flag = flag_ref[s, col] == 1
        left = rotation[:, :block]
        right_half = rotation[:, block:]
        v_send = jnp.where(flag, right_half, left)
        sends = []
        for j in range(pieces):
            vs_send[s, j] = v_send[:, j * chunk : (j + 1) * chunk]
            sends.append(launch(vs_send.at[s, j], vs_in.at[s, j], vs_sem, (s, j), right))
        vk_send[s] = jnp.where(flag, left, right_half)

        if s == 0:
            near_copy.wait_recv()
            nh[...], nm[...] = split(near0[...])
        else:
            for copy in arriving:
                copy.wait_recv()
            kept = dot3((nh[...], nm[...]), split(vk_in[s - 1]))
            nh[:, :block], nm[:, :block] = split(kept)
            for j in range(pieces):
                at = slice(block + j * chunk, block + (j + 1) * chunk)
                nh[:, at], nm[:, at] = split(near_in[s - 1, j])

        keep = dot3((ph[...], pm[...]), split(vk_send[s]))
        if s == last:
            out_ref[:, :block] = keep
        else:
            ph[:, :block], pm[:, :block] = split(keep)

        turned[...] = finish_turn(extra[...], half[...])
        mine_stat[s : s + 1] = turn_stats(turned, row, column)
        if s == last:
            tile = mine_stat[...]
            got_stat[col] = tile
            stats = [
                launch(mine_stat, got_stat.at[col], st_sem, (k - 1,), {"col": lax.rem(col + k, cols)})
                for k in range(1, cols)
            ]
        else:
            top = turned[:block, :block]
            low = turned[block:, block:]
            g[:block, :block] = jnp.where(flag, top, low)
            gs_send[s] = jnp.where(flag, low, top)

        scattered = {}
        for j in range(pieces):
            sends[j].wait_recv()
            passed = dot3((nh[...], nm[...]), split(vs_in[s, j]))
            at = slice(block + j * chunk, block + (j + 1) * chunk)
            if s == last:
                out_ref[:, at] = passed
                continue
            s_send[s, j] = passed
            ph[:, at], pm[:, at] = split(passed)
            local[s, j] = tall((ph[:, :block], pm[:, :block]), (ph[:, at], pm[:, at]))
            for i, peer in enumerate(peers):
                scattered[j, i] = launch(local.at[s, j, share(peer, block // rows)], got.at[s, j, i],
                                         ra_sem, (s, j, i), {"row": peer})
        if s == last:
            return stats
        gram_pass = launch(gs_send.at[s], gs_in.at[s], gs_sem, (s,), right)
        coming = [launch(s_send.at[s, j], near_in.at[s, j], s_sem, (s, j), right) for j in range(pieces)]
        coming.append(launch(vk_send.at[s], vk_in.at[s], vk_sem, (s,), right))
        mine = share(me, block // rows)
        gathered = []
        for j in range(pieces):
            at = slice(j * chunk, (j + 1) * chunk)
            sumd = local[s, j, mine]
            for i in range(rows - 1):
                scattered[j, i].wait_recv()
                sumd = sumd + got[s, j, i]
            cross[s, mine, at] = sumd
            for i, peer in enumerate(peers):
                spot = cross.at[s, mine, at]
                gathered.append(launch(spot, spot, rb_sem, (s, j, i), {"row": peer}))
        gram_pass.wait_recv()
        g[block:, block:] = gs_in[s]
        for copy in gathered:
            copy.wait_recv()
        g[:block, block:] = cross[s]
        g[block:, :block] = cross[s].T
        return coming

    mine_stat[...] = jnp.zeros_like(mine_stat)
    arriving = []
    for s in range(STEPS):
        arriving = step(s)
    for copy in arriving:
        copy.wait_recv()
    answer = got_stat[0]
    for k in range(1, cols):
        answer = answer + got_stat[k]
    sums_ref[...] = answer
    for copy in pending:
        copy.wait_send()


def whole_call(plan, pair):
    n, width = pair.shape
    block = width // 2
    chunk = min(block, 128)
    pieces = block // chunk
    tiles = width // chunk
    cols, rows = lax.axis_size("col"), lax.axis_size("row")
    vmem = pl.BlockSpec(memory_space=pltpu.VMEM)
    shape = jax.ShapeDtypeStruct
    dma = pltpu.SemaphoreType.DMA
    mem = pltpu.VMEM
    square = mem((width, width), f32)
    return pl.pallas_call(
        functools.partial(whole_kernel, cols, rows, chunk),
        out_shape=(shape((n, width), f32), shape((8, 128), f32)),
        in_specs=[pl.BlockSpec(memory_space=pltpu.SMEM), vmem],
        out_specs=(vmem, vmem),
        scratch_shapes=[
            square, square, square, square, square,
            mem((n, width), bf16), mem((n, width), bf16), mem((n, width), bf16), mem((n, width), bf16),
            mem((n, width), f32), mem((STEPS - 1, pieces, n, chunk), f32), mem((STEPS - 1, pieces, n, chunk), f32),
            mem((STEPS, pieces, width, chunk), f32), mem((STEPS, pieces, width, chunk), f32),
            mem((STEPS, width, block), f32), mem((STEPS - 1, width, block), f32),
            mem((STEPS - 1, block, block), f32), mem((STEPS - 1, block, block), f32),
            mem((STEPS - 1, pieces, block, chunk), f32),
            mem((STEPS - 1, pieces, rows - 1, block // rows, chunk), f32),
            mem((STEPS - 1, block, block), f32),
            mem((tiles, width, chunk), f32), mem((tiles, rows - 1, width // rows, chunk), f32), square,
            mem((8, 128), f32), mem((cols, 8, 128), f32),
            dma((2, 1)), dma((2, STEPS - 1, pieces)), dma((2, STEPS, pieces)), dma((2, STEPS - 1)),
            dma((2, STEPS - 1)), dma((2, STEPS - 1, pieces, rows - 1)), dma((2, STEPS - 1, pieces, rows - 1)),
            dma((2, tiles, rows - 1)), dma((2, tiles, rows - 1)), dma((2, cols - 1)),
        ],
        compiler_params=pltpu.CompilerParams(
            collective_id=0, has_side_effects=True, vmem_limit_bytes=56 * 1024 * 1024
        ),
        name="whole",
    )(plan, pair)


def finish_kernel(pair_ref, sums_ref, out_ref, ln_ref, sem):
    copy = pltpu.make_async_copy(pair_ref, out_ref, sem)
    copy.start()
    lane = lax.broadcasted_iota(jnp.int32, sums_ref.shape, 1)
    line = lax.broadcasted_iota(jnp.int32, sums_ref.shape, 0)
    sums = sums_ref[...]
    for s in range(STEPS):
        here = line == s
        cross_sq = jnp.sum(jnp.where(here & (lane == 0), sums, 0.0), keepdims=True)
        diag_sq = jnp.sum(jnp.where(here & (lane == 1), sums, 0.0), keepdims=True)
        ln_ref[s] = jnp.log(cross_sq / diag_sq)[0, 0]
    copy.wait()


def finish_call(pair, sums):
    vmem = pl.BlockSpec(memory_space=pltpu.VMEM)
    return pl.pallas_call(
        finish_kernel,
        out_shape=(jax.ShapeDtypeStruct(pair.shape, f32), jax.ShapeDtypeStruct((STEPS,), f32)),
        in_specs=[vmem, vmem],
        out_specs=(pl.BlockSpec(memory_space=pl.ANY), pl.BlockSpec(memory_space=pltpu.SMEM)),
        scratch_shapes=[pltpu.SemaphoreType.DMA],
        name="finish",
    )(pair, sums)


def on_device(matrix, plan):
    pair, sums = whole_call(plan, matrix)
    return finish_call(pair, sums)


def solution(mesh):
    in_specs = (P("row", "col"), P())
    out_specs = (P("row", "col"), P())
    return jax.shard_map(
        on_device, mesh=mesh, in_specs=in_specs, out_specs=out_specs, check_vma=False
    )
```

```python
import functools

import jax
import jax.numpy as jnp
from jax import lax
from jax.experimental import pallas as pl
from jax.experimental.pallas import tpu as pltpu
from jax.sharding import PartitionSpec as P

SWEEPS = 2
STEPS = 3
MESH = pl.DeviceIdType.MESH
f32 = jnp.float32
bf16 = jnp.bfloat16
eps = 1e-06
COEF = tuple(c / 6561.0 for c in (6560.0, 6544.0, 6432.0, 5984.0, 4864.0, 3072.0, 1280.0, 256.0))


def split(x):
    big = x.astype(bf16)
    return big, (x - big.astype(f32)).astype(bf16)


def dot1(a, b):
    return jnp.dot(a, b, preferred_element_type=f32)


def dot3(a, b):
    return dot1(a[0], b[0]) + (dot1(a[0], b[1]) + dot1(a[1], b[0]))


def sweep(gram, row, column):
    on_diag = row == column
    only = jnp.where(on_diag, gram, 0.0)
    d_row = jnp.sum(only, axis=0, keepdims=True)
    d_col = jnp.sum(only, axis=1, keepdims=True)
    ratio = gram / (d_col + d_row + eps)
    raw = jnp.where(row < column, ratio, jnp.where(row > column, -ratio, 0.0))
    scale = jnp.maximum(jnp.sqrt(jnp.sum(raw * raw, keepdims=True)), 1.0)
    skew = raw / scale
    parts = split(skew)
    a1 = dot1(parts[0], parts[0])
    a1b = a1.astype(bf16)
    a2 = dot1(a1b, a1b)
    a2b = a2.astype(bf16)
    a3 = dot1(a1b, a2b)
    a4 = dot1(a2b, a2b)
    low = COEF[5] * a1 + COEF[6] * a2 + COEF[7] * a3
    tail = dot1(a4.astype(bf16), low.astype(bf16))
    above = COEF[1] * a1 + COEF[2] * a2 + COEF[3] * a3 + (COEF[4] * a4 + tail)
    factor = a1 - 2.0 * skew
    extra = above + COEF[0] * factor + dot1(factor.astype(bf16), above.astype(bf16))
    extra = extra + jnp.where(on_diag, COEF[0] - 1.0, 0.0)
    part = split(extra)
    half = gram + dot3(split(gram), part)
    return extra, part, half


def finish_turn(extra, half):
    return half + dot3(split(extra.T), split(half))


def tall(first, second):
    def one(a, b):
        return lax.dot_general(a, b, (((0,), (0,)), ((), ())), preferred_element_type=f32)

    return one(first[0], second[0]) + (one(first[0], second[1]) + one(first[1], second[0]))


def remote(src, dst, send, recv, where):
    return pltpu.make_async_remote_copy(
        src_ref=src, dst_ref=dst, send_sem=send, recv_sem=recv, device_id=where, device_id_type=MESH
    )


def turn_stats(turned, row, column):
    block = turned.shape[0] // 2
    off = turned[:block, block:]
    only = jnp.where(row == column, turned[...], 0.0)
    cross_sq = jnp.sum(off * off, keepdims=True)
    diag_sq = jnp.sum(only * only, keepdims=True)
    lane = lax.broadcasted_iota(jnp.int32, (1, 128), 1)
    return jnp.where(lane == 0, cross_sq, jnp.where(lane == 1, diag_sq, 0.0))


def whole_kernel(cols, rows, chunk, tile, flag_ref, pair_ref, out_ref, sums_ref,
                 g, total, extra, half, turned, ph, pm, nh, nm, vh, vm,
                 near0, near_in, s_send, vs_send, vs_in, vk_send, vk_in, gs_send, gs_in,
                 local, got, cross, glocal, ggot, gup, mine_stat, got_stat,
                 near_sem, s_sem, vs_sem, vk_sem, vkr_sem, gs_sem, ra_sem, rb_sem, ga_sem, gb_sem, st_sem):
    width = g.shape[0]
    block = width // 2
    tall_rows = ph.shape[0]
    pieces = block // chunk
    tiles = width // chunk
    last = STEPS - 1
    col = lax.axis_index("col")
    me = lax.axis_index("row")
    right = {"col": lax.rem(col + 1, cols)}
    peers = [lax.rem(me + k, rows) for k in range(1, rows)]
    row = lax.broadcasted_iota(jnp.int32, (width, width), 0)
    column = lax.broadcasted_iota(jnp.int32, (width, width), 1)

    def share(who, whole):
        size = whole // rows
        return pl.ds(pl.multiple_of(who * size, size), size)

    def copy(src, dst, sems, at, where):
        return remote(src, dst, sems.at[(0,) + at], sems.at[(1,) + at], where)

    def to_row(i):
        return {"row": peers[i]}

    def gram_scatter(k, i):
        high = (k + 1) * chunk
        return copy(glocal.at[k, share(peers[i], high)], ggot.at[k, i, : high // rows], ga_sem, (k, i), to_row(i))

    def gram_gather(k, i):
        spot = gup.at[share(me, (k + 1) * chunk), k * chunk : (k + 1) * chunk]
        return copy(spot, spot, gb_sem, (k, i), to_row(i))

    def near_pass():
        return copy(pair_ref, near0, near_sem, (0,), right)

    def vs_pass(s, j):
        return copy(vs_send.at[s, j], vs_in.at[s, j], vs_sem, (s, j), right)

    def vk_pass(s):
        mine = share(me, width)
        return copy(vk_send.at[s, mine], vk_in.at[s, mine], vk_sem, (s,), right)

    def vk_spread(s, i):
        spot = vk_in.at[s, share(me, width)]
        return copy(spot, spot, vkr_sem, (s, i), to_row(i))

    def gs_pass(s):
        return copy(gs_send.at[s], gs_in.at[s], gs_sem, (s,), right)

    def s_pass(s, j):
        return copy(s_send.at[s, j], near_in.at[s, j], s_sem, (s, j), right)

    def cross_scatter(s, j, i):
        return copy(local.at[s, j, share(peers[i], block)], got.at[s, j, i], ra_sem, (s, j, i), to_row(i))

    def cross_gather(s, j, i):
        spot = cross.at[s, share(me, block), j * chunk : (j + 1) * chunk]
        return copy(spot, spot, rb_sem, (s, j, i), to_row(i))

    def stat_pass(k):
        return copy(mine_stat, got_stat.at[col], st_sem, (k - 1,), {"col": lax.rem(col + k, cols)})

    def each_tile(body):
        @pl.loop(0, tall_rows // tile)
        def _(t):
            body(pl.ds(pl.multiple_of(t * tile, tile), tile))

    others = range(rows - 1)

    barrier = pltpu.get_barrier_semaphore()
    for k in range(1, cols):
        pl.semaphore_signal(barrier, inc=1, device_id={"col": lax.rem(col + k, cols)}, device_id_type=MESH)
    for peer in peers:
        pl.semaphore_signal(barrier, inc=1, device_id={"row": peer}, device_id_type=MESH)

    @each_tile
    def _(at):
        ph[at], pm[at] = split(pair_ref[at])

    mine_stat[...] = jnp.zeros_like(mine_stat)
    order = list(range(tiles))[::-1]
    for n, k in enumerate(order):
        high = (k + 1) * chunk
        at = slice(k * chunk, high)
        glocal[k, :high] = tall((ph[:, :high], pm[:, :high]), (ph[:, at], pm[:, at]))
        if n == 0:
            pl.semaphore_wait(barrier, cols + rows - 2)
        for i in others:
            gram_scatter(k, i).start()
        if n == 0:
            near_pass().start()
    for k in order:
        high = (k + 1) * chunk
        mine = share(me, high)
        sumd = glocal[k, mine]
        for i in others:
            gram_scatter(k, i).wait_recv()
            sumd = sumd + ggot[k, i, : high // rows]
        gup[mine, k * chunk : high] = sumd
        for i in others:
            gram_gather(k, i).start()
    for k in order:
        for i in others:
            gram_gather(k, i).wait_recv()
    for k in range(tiles):
        at = slice(k * chunk, (k + 1) * chunk)
        for j in range(k + 1):
            to = slice(j * chunk, (j + 1) * chunk)
            square = gup[to, at]
            g[to, at] = square
            if j < k:
                g[at, to] = square.T

    @pl.loop(0, STEPS)
    def _(s):
        @pl.loop(0, SWEEPS)
        def _(turn):
            more, part, more_half = sweep(g[...], row, column)
            extra[...] = more
            half[...] = more_half

            @pl.when(turn == 0)
            def _():
                total[...] = more

            @pl.when(turn > 0)
            def _():
                before = total[...]
                total[...] = before + more + dot1(before.astype(bf16), part[0])

            @pl.when(turn + 1 < SWEEPS)
            def _():
                g[...] = finish_turn(extra[...], half[...])

        rotation = total[...] + jnp.where(row == column, 1.0, 0.0)
        flag = flag_ref[s, col] == 1
        left = rotation[:, :block]
        right_half = rotation[:, block:]
        v_send = jnp.where(flag, right_half, left)
        for j in range(pieces):
            vs_send[s, j] = v_send[:, j * chunk : (j + 1) * chunk]
            vs_pass(s, j).start()
        vk_send[s] = jnp.where(flag, left, right_half)

        turned[...] = finish_turn(extra[...], half[...])
        stat = turn_stats(turned, row, column)
        line = lax.broadcasted_iota(jnp.int32, mine_stat.shape, 0)
        mine_stat[...] = jnp.where(line == s, stat, mine_stat[...])
        top = turned[:block, :block]
        low = turned[block:, block:]
        g[:block, :block] = jnp.where(flag, top, low)

        @pl.when(s < last)
        def _():
            gs_send[s] = jnp.where(flag, low, top)

        @pl.when(s == last)
        def _():
            got_stat[col] = mine_stat[...]
            for k in range(1, cols):
                stat_pass(k).start()

        vh[...], vm[...] = split(vk_send[s])

        @pl.when(s < last)
        def _():
            @each_tile
            def _(at):
                ph[at, :block], pm[at, :block] = split(dot3((ph[at], pm[at]), (vh[...], vm[...])))

        @pl.when(s == last)
        def _():
            @each_tile
            def _(at):
                out_ref[at, :block] = dot3((ph[at], pm[at]), (vh[...], vm[...]))

        @pl.when(s == 0)
        def _():
            near_pass().wait_recv()

            @each_tile
            def _(at):
                nh[at], nm[at] = split(near0[at])

        @pl.when(s > 0)
        def _():
            for i in others:
                vk_spread(s - 1, i).wait_recv()
            vh[...], vm[...] = split(vk_in[s - 1])
            for j in range(pieces):
                s_pass(s - 1, j).wait_recv()

            @each_tile
            def _(at):
                nh[at, :block], nm[at, :block] = split(dot3((nh[at], nm[at]), (vh[...], vm[...])))
                for j in range(pieces):
                    to = slice(block + j * chunk, block + (j + 1) * chunk)
                    nh[at, to], nm[at, to] = split(near_in[s - 1, j, at])

        for j in range(pieces):
            to = slice(block + j * chunk, block + (j + 1) * chunk)
            vs_pass(s, j).wait_recv()
            vh[:, :chunk], vm[:, :chunk] = split(vs_in[s, j])

            @pl.when(s < last)
            def _():
                @each_tile
                def _(at):
                    passed = dot3((nh[at], nm[at]), (vh[:, :chunk], vm[:, :chunk]))
                    s_send[s, j, at] = passed
                    ph[at, to], pm[at, to] = split(passed)

                local[s, j] = tall((ph[:, :block], pm[:, :block]), (ph[:, to], pm[:, to]))
                for i in others:
                    cross_scatter(s, j, i).start()

            @pl.when(s == last)
            def _():
                @each_tile
                def _(at):
                    out_ref[at, to] = dot3((nh[at], nm[at]), (vh[:, :chunk], vm[:, :chunk]))

        @pl.when(s < last)
        def _():
            gs_pass(s).start()
            vk_pass(s).start()
            for j in range(pieces):
                s_pass(s, j).start()
            mine = share(me, block)
            for j in range(pieces):
                sumd = local[s, j, mine]
                for i in others:
                    cross_scatter(s, j, i).wait_recv()
                    sumd = sumd + got[s, j, i]
                cross[s, mine, j * chunk : (j + 1) * chunk] = sumd
                for i in others:
                    cross_gather(s, j, i).start()
            gs_pass(s).wait_recv()
            g[block:, block:] = gs_in[s]
            for j in range(pieces):
                for i in others:
                    cross_gather(s, j, i).wait_recv()
            g[:block, block:] = cross[s]
            g[block:, :block] = cross[s].T
            vk_pass(s).wait_recv()
            for i in others:
                vk_spread(s, i).start()

    for k in range(1, cols):
        stat_pass(k).wait_recv()
    answer = got_stat[0]
    for k in range(1, cols):
        answer = answer + got_stat[k]
    sums_ref[...] = answer
    near_pass().wait_send()
    for k in range(1, cols):
        stat_pass(k).wait_send()
    for i in others:
        for k in order:
            gram_scatter(k, i).wait_send()
            gram_gather(k, i).wait_send()

    @pl.loop(0, STEPS)
    def _(s):
        for j in range(pieces):
            vs_pass(s, j).wait_send()

    @pl.loop(0, last)
    def _(s):
        gs_pass(s).wait_send()
        vk_pass(s).wait_send()
        for i in others:
            vk_spread(s, i).wait_send()
        for j in range(pieces):
            s_pass(s, j).wait_send()
            for i in others:
                cross_scatter(s, j, i).wait_send()
                cross_gather(s, j, i).wait_send()


def whole_call(plan, pair):
    n, width = pair.shape
    block = width // 2
    chunk = min(block, 128)
    tile = min(n, 512)
    pieces = block // chunk
    tiles = width // chunk
    cols, rows = lax.axis_size("col"), lax.axis_size("row")
    last = STEPS - 1
    vmem = pl.BlockSpec(memory_space=pltpu.VMEM)
    shape = jax.ShapeDtypeStruct
    mem = pltpu.VMEM
    square = mem((width, width), f32)
    slab = mem((n, width), bf16)

    def dma(*size):
        return pltpu.SemaphoreType.DMA((2,) + size)

    return pl.pallas_call(
        functools.partial(whole_kernel, cols, rows, chunk, tile),
        out_shape=(shape((n, width), f32), shape((8, 128), f32)),
        in_specs=[pl.BlockSpec(memory_space=pltpu.SMEM), vmem],
        out_specs=(vmem, vmem),
        scratch_shapes=[
            square, square, square, square, square,
            slab, slab, slab, slab, mem((width, block), bf16), mem((width, block), bf16),
            mem((n, width), f32), mem((last, pieces, n, chunk), f32), mem((last, pieces, n, chunk), f32),
            mem((STEPS, pieces, width, chunk), f32), mem((STEPS, pieces, width, chunk), f32),
            mem((STEPS, width, block), f32), mem((last, width, block), f32),
            mem((last, block, block), f32), mem((last, block, block), f32),
            mem((last, pieces, block, chunk), f32),
            mem((last, pieces, rows - 1, block // rows, chunk), f32),
            mem((last, block, block), f32),
            mem((tiles, width, chunk), f32), mem((tiles, rows - 1, width // rows, chunk), f32), square,
            mem((8, 128), f32), mem((cols, 8, 128), f32),
            dma(1), dma(last, pieces), dma(STEPS, pieces), dma(last), dma(last, rows - 1),
            dma(last), dma(last, pieces, rows - 1), dma(last, pieces, rows - 1),
            dma(tiles, rows - 1), dma(tiles, rows - 1), dma(cols - 1),
        ],
        compiler_params=pltpu.CompilerParams(
            collective_id=0, has_side_effects=True, vmem_limit_bytes=56 * 1024 * 1024
        ),
        name="whole",
    )(plan, pair)


def finish_kernel(pair_ref, sums_ref, out_ref, ln_ref, sem):
    copy = pltpu.make_async_copy(pair_ref, out_ref, sem)
    copy.start()
    lane = lax.broadcasted_iota(jnp.int32, sums_ref.shape, 1)
    line = lax.broadcasted_iota(jnp.int32, sums_ref.shape, 0)
    sums = sums_ref[...]
    for s in range(STEPS):
        here = line == s
        cross_sq = jnp.sum(jnp.where(here & (lane == 0), sums, 0.0), keepdims=True)
        diag_sq = jnp.sum(jnp.where(here & (lane == 1), sums, 0.0), keepdims=True)
        ln_ref[s] = jnp.log(cross_sq / diag_sq)[0, 0]
    copy.wait()


def finish_call(pair, sums):
    vmem = pl.BlockSpec(memory_space=pltpu.VMEM)
    return pl.pallas_call(
        finish_kernel,
        out_shape=(jax.ShapeDtypeStruct(pair.shape, f32), jax.ShapeDtypeStruct((STEPS,), f32)),
        in_specs=[vmem, vmem],
        out_specs=(pl.BlockSpec(memory_space=pl.ANY), pl.BlockSpec(memory_space=pltpu.SMEM)),
        scratch_shapes=[pltpu.SemaphoreType.DMA],
        name="finish",
    )(pair, sums)


def on_device(matrix, plan):
    pair, sums = whole_call(plan, matrix)
    return finish_call(pair, sums)


def solution(mesh):
    in_specs = (P("row", "col"), P())
    out_specs = (P("row", "col"), P())
    return jax.shard_map(
        on_device, mesh=mesh, in_specs=in_specs, out_specs=out_specs, check_vma=False
    )
```
